256 devices in a mesh: ep: 64 (over z, x, y_hi), tp: 4 (over y_lo, core).
Axes of the slice: x: 4, y: 4 (y_hi: 2, y_lo: 2; y = y_hi * 2 + y_lo), z: 8, core: 2. Of those that a mesh axis runs over, the one named last changes fastest.
Arguments:
- context: bfloat16 [8192, 4096], P('ep', 'tp'), may hold values from -6 to 6
- wo_proj: bfloat16 [4096, 4096], P('tp'), may hold values from -0.09375 to 0.09375
- residual: bfloat16 [8192, 4096], P(('ep', 'tp')), may hold values from -16 to 16
- norm_gain: bfloat16 [4096], replicated, may hold values from 0.25 to 1.75
- expert_ids: int32 [8192, 8], P(('ep', 'tp')), may hold values from 0 to 63, all different within a row; in each aligned block of 32 rows (0 to 31, 32 to 63, ...) at most 8 rows name the same one
- route_weights: float32 [8192, 8], P(('ep', 'tp')), may hold values from 0.1 to 1
- w_gate_up: bfloat16 [64, 2, 768, 4096], P('ep', None, 'tp'), may hold values from -0.09375 to 0.09375
- w_down: bfloat16 [64, 768, 4096], P('ep', 'tp'), may hold values from -0.21875 to 0.21875
Outputs:
- layer_out: bfloat16 [8192, 4096], P(('ep', 'tp'))
The draws below stay inside these ranges and needn't reach their ends.
Inputs may be any that keep to these rules, and one draw needn't show every extreme that they name: `expert_ids`: within the routes of one device's 32 tokens no expert is named more than 8 times, a bound that some block reaches; a token names 8 different experts.
All inputs are finite; a program needn't handle non-finite values.
Results may differ from the reference program's by a relative error of at most 0.0085.
Values may be sent and summed in bfloat16 or wider, within the bound.
A program may use at most 128 MiB of HBM per device.

```python
import math
import jax
import jax.numpy as jnp
import numpy as np
from jax import lax

D = 4096
HEADS = 32
HD = 128
FFE = 768
TOPK = 8
EXPERTS = 64
TOK_Q = 32
TOKENS = 8192
CAP = 8
N_TP = 4


def draw_residual(key, part):
    key_base, key_columns, key_scale = jax.random.split(key, 3)
    entries = jnp.clip(jax.random.normal(key_base, (TOKENS, D), jnp.float32), -4.0, 4.0)
    row_scale = jnp.exp(jax.random.uniform(key_scale, (TOKENS, 1), jnp.float32, math.log(0.5), math.log(2.0)))
    column_scale = jnp.exp(jax.random.uniform(key_columns, (1, D), jnp.float32, math.log(0.2), math.log(2.0)))
    return (entries * column_scale * row_scale).astype(jnp.bfloat16)


def levels(rng, extent, pieces, low, largest):
    gain = 1.0
    for dim, parts in pieces:
        draws = jax.random.uniform(jax.random.fold_in(jax.random.fold_in(rng, 6), dim), (parts,), jnp.float32, low / len(pieces), largest / len(pieces))
        gain = gain * jnp.repeat(jnp.exp(draws), extent[dim] // parts).reshape((-1,) + (1,) * (len(extent) - 1 - dim))
    return gain


def assign_block(key, own, number, rows, count, top, bound, slope):
    sequence = jax.random.permutation(key, count)
    heavy_load, ordinary = load_shares(count, rows * top, bound, slope, True), load_shares(count, rows * top, bound, slope, False)
    places = jnp.arange(count)

    def named(lengths, rotation):
        used = int((lengths > 0).sum())
        fixed = max(1, used // 4)
        moved = fixed + (places - fixed + rotation * (used - fixed)) % max(1, count - fixed)
        return jnp.zeros((count,), jnp.int32).at[sequence[jnp.where(places < fixed, places, moved)]].set(jnp.asarray(lengths, jnp.int32))

    lengths = jnp.where(number % 4 == 0, named(heavy_load, number // 4), named(ordinary, number - number // 4 - 1))
    mixed = jax.random.permutation(jax.random.fold_in(own, 3), count)
    giver, taker = mixed[0:count // 2 * 2:2], mixed[1:count // 2 * 2:2]
    slack = jnp.minimum(lengths[giver] - 1, bound - lengths[taker]) // 2
    slack = jnp.where((giver == sequence[0]) | (taker == sequence[0]) | (lengths[taker] == 0), 0, jnp.maximum(slack, 0))
    moved = jax.random.randint(jax.random.fold_in(own, 4), (count // 2,), 0, 1 << 20) % (slack + 1)
    lengths = lengths.at[giver].add(-moved).at[taker].add(moved)
    items = jnp.searchsorted(jnp.cumsum(lengths), jnp.arange(rows * top), side="right").astype(jnp.int32)
    grid = items.reshape(top, rows).T
    grid = grid[jax.random.permutation(jax.random.fold_in(own, 1), rows)]
    rotation = jax.random.randint(jax.random.fold_in(own, 2), (rows, 1), 0, top)
    return jnp.take_along_axis(grid, (jnp.arange(top)[None, :] + rotation) % top, axis=1)


def load_shares(amount, total, reach, lean, full):
    portions = [(1 << 20) // math.isqrt(standing ** lean) + 1 for standing in range(1, amount + 1)]
    largest = reach if full else min(reach, max(-(-total // amount), total * portions[0] // sum(portions)))
    least = 1 if total - largest >= amount - 1 else 0
    given, surplus = [largest] + [least] * (amount - 1), total - largest - least * (amount - 1)
    while surplus > 0:
        candidates = [i for i in range(1, amount) if given[i] < largest] or [i for i in range(1, amount) if given[i] < reach]
        mass, left = sum([portions[i] for i in candidates]), surplus
        for i in candidates:
            extra = min(reach - given[i], max(1, left * portions[i] // mass), surplus)
            given[i] = given[i] + extra
            surplus = surplus - extra
    return np.array(given)


def centred(own_key, extent, deviation, most, pieces=(), held_as=jnp.bfloat16):
    drawn = deviation * jax.random.normal(own_key, extent, jnp.float32)
    if pieces:
        drawn = drawn * levels(own_key, extent, pieces, -0.22, 0.18)
    return jnp.clip(drawn, -most, most).astype(held_as)


def setup_inputs(seed: int = 0) -> dict:
    seeds = jax.random.split(jax.random.key(seed), 9)
    context = centred(seeds[0], (TOKENS, HEADS * HD), 1.0, 6.0, ((0, 64), (1, 4)))
    wo_proj = centred(seeds[1], (HEADS * HD, D), (HEADS * HD) ** -0.5, 0.09375, ((0, 4),))
    residual = draw_residual(jax.random.fold_in(seeds[8], 71), 0)
    norm_gain = jnp.clip(1.0 + 0.15 * jax.random.normal(seeds[3], (D,), jnp.float32), 0.25, 1.75).astype(jnp.bfloat16)
    expert_ids_keys = jax.random.split(jax.random.fold_in(seeds[4], 1), TOKENS // TOK_Q)
    expert_ids_turns = jax.random.permutation(jax.random.fold_in(seeds[4], 3), TOKENS // TOK_Q)
    expert_ids = jax.vmap(lambda own, number: assign_block(jax.random.fold_in(seeds[4], 2), own, number, TOK_Q, EXPERTS, TOPK, CAP, 2))(expert_ids_keys, expert_ids_turns).reshape((TOKENS, TOPK))
    route_weights = jnp.clip(0.1 + 0.9 * jax.random.uniform(seeds[5], (TOKENS, TOPK), jnp.float32) ** levels(seeds[5], (TOKENS, TOPK), ((0, 256),), -0.2, 0.2), 0.1, 1.0)
    w_gate_up = centred(seeds[6], (EXPERTS, 2, FFE, D), D ** -0.5, 0.09375, ((0, 64), (2, 4)))
    w_down = centred(seeds[7], (EXPERTS, FFE, D), FFE ** -0.5, 0.21875, ((0, 64), (1, 4)))
    return dict(context=context, wo_proj=wo_proj, residual=residual, norm_gain=norm_gain, expert_ids=expert_ids, route_weights=route_weights, w_gate_up=w_gate_up, w_down=w_down)


def reference(context, wo_proj, residual, norm_gain, expert_ids, route_weights, w_gate_up, w_down):
    attn = jnp.dot(context, wo_proj, preferred_element_type=jnp.float32)
    hidden = residual.astype(jnp.float32) + attn
    inverse_rms = lax.rsqrt(lax.optimization_barrier(jnp.mean(hidden * hidden, axis=1, keepdims=True)) + 1e-06)
    normed = (hidden * inverse_rms * norm_gain.astype(jnp.float32)).astype(jnp.bfloat16)
    group_count = TOKENS // TOK_Q
    group_rows = TOK_Q * TOPK
    grouped_ids = expert_ids.reshape(group_count, group_rows)
    onehot = (grouped_ids[:, :, None] == jnp.arange(EXPERTS, dtype=jnp.int32)[None, None, :]).astype(jnp.int32)
    before = jnp.cumsum(onehot, axis=1, dtype=jnp.int32) - onehot
    position = lax.optimization_barrier(jnp.sum(before * onehot, axis=2, dtype=jnp.int32))
    slot_index = jnp.arange(group_count, dtype=jnp.int32)[:, None] * CAP + position
    route_index = jnp.arange(TOKENS * TOPK, dtype=jnp.int32).reshape(group_count, group_rows)
    table = jnp.full((EXPERTS, group_count * CAP), TOKENS * TOPK, dtype=jnp.int32)
    table = table.at[grouped_ids.reshape(-1), slot_index.reshape(-1)].set(route_index.reshape(-1))
    normed_ext = jnp.concatenate([normed, jnp.zeros((1, D), jnp.bfloat16)], axis=0)
    weight_ext = jnp.concatenate([route_weights.reshape(-1), jnp.zeros((1,), jnp.float32)], axis=0)
    quarter = FFE // N_TP

    def expert_step(summed, inputs):
        routes, weight_in, weight_out = inputs
        token_index = routes // TOPK
        gathered = normed_ext[token_index]
        gate = lax.dot_general(gathered, weight_in[0], (((1,), (1,)), ((), ())), preferred_element_type=jnp.float32)
        up_proj = lax.dot_general(gathered, weight_in[1], (((1,), (1,)), ((), ())), preferred_element_type=jnp.float32)
        activated = (jax.nn.silu(gate) * up_proj).astype(jnp.bfloat16)
        combined = jnp.zeros((gathered.shape[0], D), jnp.float32)
        for section in range(N_TP):
            part_sum = jnp.dot(activated[:, section * quarter:(section + 1) * quarter], weight_out[section * quarter:(section + 1) * quarter], preferred_element_type=jnp.float32).astype(jnp.bfloat16)
            part_sum = lax.optimization_barrier(part_sum)
            combined = combined + part_sum.astype(jnp.float32)
        expert_out = combined.astype(jnp.bfloat16)
        weighted = weight_ext[routes][:, None] * expert_out.astype(jnp.float32)
        summed = summed.at[token_index].add(weighted)
        return (summed, None)
    start_sum = jnp.zeros((TOKENS + 1, D), jnp.float32)
    summed, _ = lax.scan(expert_step, start_sum, (table, w_gate_up, w_down))
    return (hidden + summed[:TOKENS]).astype(jnp.bfloat16)
```

```python
import jax
import jax.numpy as jnp
from jax import lax
from jax.sharding import PartitionSpec as P


def local(context, wo_proj, residual, norm_gain, expert_ids, route_weights, w_gate_up, w_down):
    quarter_rows, model_width = residual.shape
    top_count = expert_ids.shape[1]
    exp_local = w_gate_up.shape[0]
    ep_size = lax.axis_size("ep")
    experts = exp_local * ep_size
    capacity = max(2, min(quarter_rows, 2 * quarter_rows * top_count // experts))
    gate_up_full = lax.all_gather(w_gate_up, "tp", axis=2, tiled=True)
    down_full = lax.all_gather(w_down, "tp", axis=1, tiled=True)
    attn = lax.psum_scatter(
        jnp.dot(context, wo_proj, preferred_element_type=jnp.float32),
        "tp",
        scatter_dimension=0,
        tiled=True,
    )
    hidden = residual.astype(jnp.float32) + attn
    inverse_rms = lax.rsqrt(jnp.mean(hidden * hidden, axis=1, keepdims=True) + 1e-06)
    normed = (hidden * inverse_rms * norm_gain.astype(jnp.float32)).astype(jnp.bfloat16)
    flat_ids = expert_ids.reshape(-1)
    onehot = (flat_ids[:, None] == jnp.arange(experts, dtype=jnp.int32)[None, :]).astype(jnp.int32)
    before = jnp.cumsum(onehot, axis=0, dtype=jnp.int32) - onehot
    position = jnp.sum(before * onehot, axis=1, dtype=jnp.int32)
    slot_ids = flat_ids * capacity + position
    slot_range = jnp.arange(experts * capacity, dtype=jnp.int32)
    selected = slot_range[:, None] == slot_ids[None, :]
    placement = jnp.any(
        selected.reshape(experts * capacity, quarter_rows, top_count), axis=2
    ).astype(jnp.bfloat16)
    send_rows = jnp.dot(placement, normed, preferred_element_type=jnp.float32).astype(jnp.bfloat16)
    send_rows = send_rows.reshape(ep_size, exp_local * capacity, model_width)
    received = lax.all_to_all(send_rows, "ep", split_axis=0, concat_axis=0, tiled=True)
    received = received.reshape(ep_size, exp_local, capacity, model_width)
    gate = jnp.einsum(
        "sjcd,jfd->sjcf", received, gate_up_full[:, 0], preferred_element_type=jnp.float32
    )
    up_proj = jnp.einsum(
        "sjcd,jfd->sjcf", received, gate_up_full[:, 1], preferred_element_type=jnp.float32
    )
    activated = (jax.nn.silu(gate) * up_proj).astype(jnp.bfloat16)
    expert_out = jnp.einsum(
        "sjcf,jfd->sjcd", activated, down_full, preferred_element_type=jnp.float32
    ).astype(jnp.bfloat16)
    returned = lax.all_to_all(
        expert_out.reshape(ep_size, exp_local * capacity, model_width),
        "ep",
        split_axis=0,
        concat_axis=0,
        tiled=True,
    )
    returned = returned.reshape(experts * capacity, model_width)
    token_slots = slot_ids.reshape(quarter_rows, top_count)
    mixture = jnp.zeros((quarter_rows, model_width), jnp.float32)
    for choice_index in range(top_count):
        picker = (slot_range[None, :] == token_slots[:, choice_index][:, None]).astype(jnp.bfloat16)
        picked = jnp.dot(picker, returned, preferred_element_type=jnp.float32)
        mixture = mixture + route_weights[:, choice_index : choice_index + 1] * picked
    return (hidden + mixture).astype(jnp.bfloat16)


def solution(mesh):
    in_specs = (
        P("ep", "tp"),
        P("tp", None),
        P(("ep", "tp"), None),
        P(),
        P(("ep", "tp"), None),
        P(("ep", "tp"), None),
        P("ep", None, "tp", None),
        P("ep", "tp", None),
    )
    out_specs = P(("ep", "tp"), None)
    return jax.shard_map(local, mesh=mesh, in_specs=in_specs, out_specs=out_specs, check_vma=False)
```

```python
import jax
import jax.numpy as jnp
from jax import lax
from jax.sharding import PartitionSpec as P


def gather_weights(w_gate_up, w_down):
    tp_size = lax.axis_size("tp")
    half = tp_size // 2
    far_pairs = [(j, j ^ half) for j in range(tp_size)]
    near_pairs = [(j, j ^ 1) for j in range(tp_size)]
    own = (w_gate_up, w_down)
    far = lax.ppermute(own, "tp", far_pairs)
    near_own, near_far = lax.ppermute((own, far), "tp", near_pairs)
    return [own, far, near_own, near_far]


def local(context, wo_proj, residual, norm_gain, expert_ids, route_weights, w_gate_up, w_down):
    quarter_rows, model_width = residual.shape
    top_count = expert_ids.shape[1]
    exp_local = w_gate_up.shape[0]
    ep_size = lax.axis_size("ep")
    experts = exp_local * ep_size
    capacity = max(2, min(quarter_rows, 2 * quarter_rows * top_count // experts))
    pieces = gather_weights(w_gate_up, w_down)
    attn = lax.psum_scatter(
        jnp.dot(context, wo_proj, preferred_element_type=jnp.float32),
        "tp",
        scatter_dimension=0,
        tiled=True,
    )
    hidden = residual.astype(jnp.float32) + attn
    inverse_rms = lax.rsqrt(jnp.mean(hidden * hidden, axis=1, keepdims=True) + 1e-06)
    normed = (hidden * inverse_rms * norm_gain.astype(jnp.float32)).astype(jnp.bfloat16)
    flat_ids = expert_ids.reshape(-1)
    onehot = (flat_ids[:, None] == jnp.arange(experts, dtype=jnp.int32)[None, :]).astype(jnp.int32)
    before = jnp.cumsum(onehot, axis=0, dtype=jnp.int32) - onehot
    position = jnp.sum(before * onehot, axis=1, dtype=jnp.int32)
    slot_ids = flat_ids * capacity + position
    slot_range = jnp.arange(experts * capacity, dtype=jnp.int32)
    selected = slot_range[:, None] == slot_ids[None, :]
    placement = jnp.any(
        selected.reshape(experts * capacity, quarter_rows, top_count), axis=2
    ).astype(jnp.bfloat16)
    send_rows = jnp.dot(placement, normed, preferred_element_type=jnp.float32).astype(jnp.bfloat16)
    send_rows = send_rows.reshape(ep_size, exp_local * capacity, model_width)
    received = lax.all_to_all(send_rows, "ep", split_axis=0, concat_axis=0, tiled=True)
    received = received.reshape(ep_size, exp_local, capacity, model_width)
    activated = []
    for gate_up_piece, _ in pieces:
        both = jnp.einsum(
            "sjcd,jgfd->sjcgf", received, gate_up_piece, preferred_element_type=jnp.float32
        )
        activated.append((jax.nn.silu(both[:, :, :, 0]) * both[:, :, :, 1]).astype(jnp.bfloat16))
    activated = jnp.concatenate(activated, axis=3)
    down_full = jnp.concatenate([down_piece for _, down_piece in pieces], axis=1)
    expert_out = jnp.einsum(
        "sjcf,jfd->sjcd", activated, down_full, preferred_element_type=jnp.float32
    ).astype(jnp.bfloat16)
    returned = lax.all_to_all(
        expert_out.reshape(ep_size, exp_local * capacity, model_width),
        "ep",
        split_axis=0,
        concat_axis=0,
        tiled=True,
    )
    returned = returned.reshape(experts * capacity, model_width)
    token_slots = slot_ids.reshape(quarter_rows, top_count)
    combine = jnp.zeros((quarter_rows, experts * capacity), jnp.float32)
    for choice_index in range(top_count):
        hit = slot_range[None, :] == token_slots[:, choice_index][:, None]
        combine = combine + jnp.where(hit, route_weights[:, choice_index : choice_index + 1], 0.0)
    combine_hi = combine.astype(jnp.bfloat16)
    combine_lo = (combine - combine_hi.astype(jnp.float32)).astype(jnp.bfloat16)
    picked = jnp.dot(
        jnp.concatenate([combine_hi, combine_lo], axis=0), returned, preferred_element_type=jnp.float32
    )
    mixture = picked[:quarter_rows] + picked[quarter_rows:]
    return (hidden + mixture).astype(jnp.bfloat16)


def solution(mesh):
    in_specs = (
        P("ep", "tp"),
        P("tp", None),
        P(("ep", "tp"), None),
        P(),
        P(("ep", "tp"), None),
        P(("ep", "tp"), None),
        P("ep", None, "tp", None),
        P("ep", "tp", None),
    )
    out_specs = P(("ep", "tp"), None)
    return jax.shard_map(local, mesh=mesh, in_specs=in_specs, out_specs=out_specs, check_vma=False)
```

```python
import jax
import jax.numpy as jnp
from jax import lax
from jax.sharding import PartitionSpec as P


def gather_weights(w_gate_up, w_down):
    tp_size = lax.axis_size("tp")
    half = tp_size // 2
    far_pairs = [(j, j ^ half) for j in range(tp_size)]
    near_pairs = [(j, j ^ 1) for j in range(tp_size)]
    own = (w_gate_up, w_down)
    far = lax.ppermute(own, "tp", far_pairs)
    near_own, near_far = lax.ppermute((own, far), "tp", near_pairs)
    return [own, far, near_own, near_far]


def layer(context, wo_proj, residual, norm_gain, expert_ids, route_weights, w_gate_up, w_down):
    quarter_rows, model_width = residual.shape
    top_count = expert_ids.shape[1]
    exp_local = w_gate_up.shape[0]
    ep_size = lax.axis_size("ep")
    experts = exp_local * ep_size
    capacity = max(2, min(quarter_rows, 2 * quarter_rows * top_count // experts))
    pieces = gather_weights(w_gate_up, w_down)
    attn_part = jnp.dot(context, wo_proj, preferred_element_type=jnp.float32)
    attn = lax.psum_scatter(
        attn_part,
        "tp",
        scatter_dimension=0,
        tiled=True,
    )
    hidden = residual.astype(jnp.float32) + attn
    inverse_rms = lax.rsqrt(jnp.mean(hidden * hidden, axis=1, keepdims=True) + 1e-06)
    normed = (hidden * inverse_rms * norm_gain.astype(jnp.float32)).astype(jnp.bfloat16)
    flat_ids = expert_ids.reshape(-1)
    onehot = (flat_ids[:, None] == jnp.arange(experts, dtype=jnp.int32)[None, :]).astype(jnp.int32)
    before = jnp.cumsum(onehot, axis=0, dtype=jnp.int32) - onehot
    position = jnp.sum(before * onehot, axis=1, dtype=jnp.int32)
    slot_ids = flat_ids * capacity + position
    slot_range = jnp.arange(experts * capacity, dtype=jnp.int32)
    selected = slot_range[:, None] == slot_ids[None, :]
    placement = jnp.any(
        selected.reshape(experts * capacity, quarter_rows, top_count), axis=2
    ).astype(jnp.bfloat16)
    send_rows = jnp.dot(placement, normed, preferred_element_type=jnp.float32).astype(jnp.bfloat16)
    send_rows = send_rows.reshape(ep_size, exp_local * capacity, model_width)
    received = lax.all_to_all(send_rows, "ep", split_axis=0, concat_axis=0, tiled=True)
    received = received.reshape(ep_size, exp_local, capacity, model_width)
    slots = ep_size * exp_local * capacity
    rows = received.reshape(slots, model_width)
    gate_up_full = jnp.concatenate(
        [piece.reshape(-1, model_width) for piece, _ in pieces], axis=0
    )
    down_full = jnp.concatenate([piece.reshape(-1, model_width) for _, piece in pieces], axis=0)
    both = jnp.dot(rows, gate_up_full.T, preferred_element_type=jnp.float32)
    both = both.reshape(slots, len(pieces), 2, -1)
    activated = (jax.nn.silu(both[:, :, 0]) * both[:, :, 1]).astype(jnp.bfloat16)
    expert_out = jnp.dot(
        activated.reshape(slots, -1), down_full, preferred_element_type=jnp.float32
    ).astype(jnp.bfloat16)
    returned = lax.all_to_all(
        expert_out.reshape(ep_size, exp_local * capacity, model_width),
        "ep",
        split_axis=0,
        concat_axis=0,
        tiled=True,
    )
    returned = returned.reshape(experts * capacity, model_width)
    token_slots = slot_ids.reshape(quarter_rows, top_count)
    combine = jnp.zeros((quarter_rows, experts * capacity), jnp.float32)
    for choice_index in range(top_count):
        hit = slot_range[None, :] == token_slots[:, choice_index][:, None]
        combine = combine + jnp.where(hit, route_weights[:, choice_index : choice_index + 1], 0.0)
    combine_hi = combine.astype(jnp.bfloat16)
    combine_lo = (combine - combine_hi.astype(jnp.float32)).astype(jnp.bfloat16)
    picked = jnp.dot(
        jnp.concatenate([combine_hi, combine_lo], axis=0), returned, preferred_element_type=jnp.float32
    )
    mixture = picked[:quarter_rows] + picked[quarter_rows:]
    return (hidden + mixture).astype(jnp.bfloat16)


def solution(mesh):
    in_specs = (
        P("ep", "tp"),
        P("tp", None),
        P(("ep", "tp"), None),
        P(),
        P(("ep", "tp"), None),
        P(("ep", "tp"), None),
        P("ep", None, "tp", None),
        P("ep", "tp", None),
    )
    out_specs = P(("ep", "tp"), None)
    return jax.shard_map(layer, mesh=mesh, in_specs=in_specs, out_specs=out_specs, check_vma=False)
```

```python
import jax
import jax.numpy as jnp
from jax import lax
from jax.sharding import PartitionSpec as P


def gather_weights(w_gate_up, w_down):
    tp_size = lax.axis_size("tp")
    half = tp_size // 2
    far_pairs = [(j, j ^ half) for j in range(tp_size)]
    near_pairs = [(j, j ^ 1) for j in range(tp_size)]
    own = (w_gate_up, w_down)
    far = lax.ppermute(own, "tp", far_pairs)
    near_own, near_far = lax.ppermute((own, far), "tp", near_pairs)
    return [own, far, near_own, near_far]


def layer(context, wo_proj, residual, norm_gain, expert_ids, route_weights, w_gate_up, w_down):
    quarter_rows, model_width = residual.shape
    top_count = expert_ids.shape[1]
    exp_local = w_gate_up.shape[0]
    ep_size = lax.axis_size("ep")
    experts = exp_local * ep_size
    capacity = max(2, min(quarter_rows, 2 * quarter_rows * top_count // experts))
    pieces = gather_weights(w_gate_up, w_down)
    attn_part = jnp.dot(context, wo_proj, preferred_element_type=jnp.float32)
    tp_size = lax.axis_size("tp")
    shares = attn_part.astype(jnp.bfloat16).reshape(tp_size, quarter_rows, model_width)
    shares = lax.all_to_all(shares, "tp", split_axis=0, concat_axis=0, tiled=True)
    attn = jnp.sum(shares.astype(jnp.float32), axis=0)
    hidden = residual.astype(jnp.float32) + attn
    inverse_rms = lax.rsqrt(jnp.mean(hidden * hidden, axis=1, keepdims=True) + 1e-06)
    normed = (hidden * inverse_rms * norm_gain.astype(jnp.float32)).astype(jnp.bfloat16)
    flat_ids = expert_ids.reshape(-1)
    onehot = (flat_ids[:, None] == jnp.arange(experts, dtype=jnp.int32)[None, :]).astype(jnp.int32)
    before = jnp.cumsum(onehot, axis=0, dtype=jnp.int32) - onehot
    position = jnp.sum(before * onehot, axis=1, dtype=jnp.int32)
    slot_ids = flat_ids * capacity + position
    slot_range = jnp.arange(experts * capacity, dtype=jnp.int32)
    selected = slot_range[:, None] == slot_ids[None, :]
    placement = jnp.any(
        selected.reshape(experts * capacity, quarter_rows, top_count), axis=2
    ).astype(jnp.bfloat16)
    send_rows = jnp.dot(placement, normed, preferred_element_type=jnp.float32).astype(jnp.bfloat16)
    send_rows = send_rows.reshape(ep_size, exp_local * capacity, model_width)
    received = lax.all_to_all(send_rows, "ep", split_axis=0, concat_axis=0, tiled=True)
    received = received.reshape(ep_size, exp_local, capacity, model_width)
    slots = ep_size * exp_local * capacity
    rows = received.reshape(slots, model_width)
    gate_up_full = jnp.concatenate(
        [piece.reshape(-1, model_width) for piece, _ in pieces], axis=0
    )
    down_full = jnp.concatenate([piece.reshape(-1, model_width) for _, piece in pieces], axis=0)
    both = jnp.dot(rows, gate_up_full.T, preferred_element_type=jnp.float32)
    both = both.reshape(slots, len(pieces), 2, -1)
    activated = (jax.nn.silu(both[:, :, 0]) * both[:, :, 1]).astype(jnp.bfloat16)
    expert_out = jnp.dot(
        activated.reshape(slots, -1), down_full, preferred_element_type=jnp.float32
    ).astype(jnp.bfloat16)
    returned = lax.all_to_all(
        expert_out.reshape(ep_size, exp_local * capacity, model_width),
        "ep",
        split_axis=0,
        concat_axis=0,
        tiled=True,
    )
    returned = returned.reshape(experts * capacity, model_width)
    token_slots = slot_ids.reshape(quarter_rows, top_count)
    combine = jnp.zeros((quarter_rows, experts * capacity), jnp.float32)
    for choice_index in range(top_count):
        hit = slot_range[None, :] == token_slots[:, choice_index][:, None]
        combine = combine + jnp.where(hit, route_weights[:, choice_index : choice_index + 1], 0.0)
    combine_hi = combine.astype(jnp.bfloat16)
    combine_lo = (combine - combine_hi.astype(jnp.float32)).astype(jnp.bfloat16)
    picked = jnp.dot(
        jnp.concatenate([combine_hi, combine_lo], axis=0), returned, preferred_element_type=jnp.float32
    )
    mixture = picked[:quarter_rows] + picked[quarter_rows:]
    return (hidden + mixture).astype(jnp.bfloat16)


def solution(mesh):
    in_specs = (
        P("ep", "tp"),
        P("tp", None),
        P(("ep", "tp"), None),
        P(),
        P(("ep", "tp"), None),
        P(("ep", "tp"), None),
        P("ep", None, "tp", None),
        P("ep", "tp", None),
    )
    out_specs = P(("ep", "tp"), None)
    return jax.shard_map(layer, mesh=mesh, in_specs=in_specs, out_specs=out_specs, check_vma=False)
```

```python
import jax
import jax.numpy as jnp
from jax import lax
from jax.sharding import PartitionSpec as P


def gather_weights(w_gate_up, w_down):
    tp_size = lax.axis_size("tp")
    half = tp_size // 2
    far_pairs = [(j, j ^ half) for j in range(tp_size)]
    near_pairs = [(j, j ^ 1) for j in range(tp_size)]
    own = (w_gate_up, w_down)
    far = lax.ppermute(own, "tp", far_pairs)
    near_own = lax.ppermute(own, "tp", near_pairs)
    near_far = lax.ppermute(far, "tp", near_pairs)
    return [own, far, near_own, near_far]


def layer(context, wo_proj, residual, norm_gain, expert_ids, route_weights, w_gate_up, w_down):
    quarter_rows, model_width = residual.shape
    top_count = expert_ids.shape[1]
    exp_local = w_gate_up.shape[0]
    ep_size = lax.axis_size("ep")
    experts = exp_local * ep_size
    capacity = max(2, min(quarter_rows, 2 * quarter_rows * top_count // experts))
    pieces = gather_weights(w_gate_up, w_down)
    attn_part = jnp.dot(context, wo_proj, preferred_element_type=jnp.float32)
    attn = lax.psum_scatter(
        attn_part.astype(jnp.bfloat16),
        "tp",
        scatter_dimension=0,
        tiled=True,
    ).astype(jnp.float32)
    hidden = residual.astype(jnp.float32) + attn
    inverse_rms = lax.rsqrt(jnp.mean(hidden * hidden, axis=1, keepdims=True) + 1e-06)
    normed = (hidden * inverse_rms * norm_gain.astype(jnp.float32)).astype(jnp.bfloat16)
    flat_ids = expert_ids.reshape(-1)
    onehot = (flat_ids[:, None] == jnp.arange(experts, dtype=jnp.int32)[None, :]).astype(jnp.int32)
    before = jnp.cumsum(onehot, axis=0, dtype=jnp.int32) - onehot
    position = jnp.sum(before * onehot, axis=1, dtype=jnp.int32)
    slot_ids = flat_ids * capacity + position
    slot_range = jnp.arange(experts * capacity, dtype=jnp.int32)
    selected = slot_range[:, None] == slot_ids[None, :]
    placement = jnp.any(
        selected.reshape(experts * capacity, quarter_rows, top_count), axis=2
    ).astype(jnp.bfloat16)
    send_rows = jnp.dot(placement, normed, preferred_element_type=jnp.float32).astype(jnp.bfloat16)
    send_rows = send_rows.reshape(ep_size, exp_local * capacity, model_width)
    received = lax.all_to_all(send_rows, "ep", split_axis=0, concat_axis=0, tiled=True)
    received = received.reshape(ep_size, exp_local, capacity, model_width)
    slots = ep_size * exp_local * capacity
    rows = received.reshape(slots, model_width)
    gate_up_full = jnp.concatenate(
        [piece.reshape(-1, model_width) for piece, _ in pieces], axis=0
    )
    down_full = jnp.concatenate([piece.reshape(-1, model_width) for _, piece in pieces], axis=0)
    both = jnp.dot(rows, gate_up_full.T, preferred_element_type=jnp.float32)
    both = both.reshape(slots, len(pieces), 2, -1)
    activated = (jax.nn.silu(both[:, :, 0]) * both[:, :, 1]).astype(jnp.bfloat16)
    expert_out = jnp.dot(
        activated.reshape(slots, -1), down_full, preferred_element_type=jnp.float32
    ).astype(jnp.bfloat16)
    returned = lax.all_to_all(
        expert_out.reshape(ep_size, exp_local * capacity, model_width),
        "ep",
        split_axis=0,
        concat_axis=0,
        tiled=True,
    )
    returned = returned.reshape(experts * capacity, model_width)
    token_slots = slot_ids.reshape(quarter_rows, top_count)
    combine = jnp.zeros((quarter_rows, experts * capacity), jnp.float32)
    for choice_index in range(top_count):
        hit = slot_range[None, :] == token_slots[:, choice_index][:, None]
        combine = combine + jnp.where(hit, route_weights[:, choice_index : choice_index + 1], 0.0)
    combine_hi = combine.astype(jnp.bfloat16)
    combine_lo = (combine - combine_hi.astype(jnp.float32)).astype(jnp.bfloat16)
    picked = jnp.dot(
        jnp.concatenate([combine_hi, combine_lo], axis=0), returned, preferred_element_type=jnp.float32
    )
    mixture = picked[:quarter_rows] + picked[quarter_rows:]
    return (hidden + mixture).astype(jnp.bfloat16)


def solution(mesh):
    in_specs = (
        P("ep", "tp"),
        P("tp", None),
        P(("ep", "tp"), None),
        P(),
        P(("ep", "tp"), None),
        P(("ep", "tp"), None),
        P("ep", None, "tp", None),
        P("ep", "tp", None),
    )
    out_specs = P(("ep", "tp"), None)
    return jax.shard_map(layer, mesh=mesh, in_specs=in_specs, out_specs=out_specs, check_vma=False)
```

```python
import jax
import jax.numpy as jnp
from jax import lax
from jax.sharding import PartitionSpec as P


def gather_weights(w_gate_up, w_down):
    tp_size = lax.axis_size("tp")
    half = tp_size // 2
    far_pairs = [(j, j ^ half) for j in range(tp_size)]
    near_pairs = [(j, j ^ 1) for j in range(tp_size)]
    own = (w_gate_up, w_down)
    far = lax.ppermute(own, "tp", far_pairs)
    near_own = lax.ppermute(own, "tp", near_pairs)
    near_far = lax.ppermute(far, "tp", near_pairs)
    return [own, far, near_own, near_far]


def layer(context, wo_proj, residual, norm_gain, expert_ids, route_weights, w_gate_up, w_down):
    quarter_rows, model_width = residual.shape
    top_count = expert_ids.shape[1]
    exp_local = w_gate_up.shape[0]
    ep_size = lax.axis_size("ep")
    experts = exp_local * ep_size
    capacity = max(2, min(quarter_rows, 2 * quarter_rows * top_count // experts))
    pieces = gather_weights(w_gate_up, w_down)
    attn_part = jnp.dot(context, wo_proj, preferred_element_type=jnp.float32)
    attn = lax.psum_scatter(
        attn_part.astype(jnp.bfloat16),
        "tp",
        scatter_dimension=0,
        tiled=True,
    ).astype(jnp.float32)
    hidden = residual.astype(jnp.float32) + attn
    inverse_rms = lax.rsqrt(jnp.mean(hidden * hidden, axis=1, keepdims=True) + 1e-06)
    normed = (hidden * inverse_rms * norm_gain.astype(jnp.float32)).astype(jnp.bfloat16)
    flat_ids = expert_ids.reshape(-1)
    onehot = (flat_ids[:, None] == jnp.arange(experts, dtype=jnp.int32)[None, :]).astype(jnp.int32)
    before = jnp.cumsum(onehot, axis=0, dtype=jnp.int32) - onehot
    position = jnp.sum(before * onehot, axis=1, dtype=jnp.int32)
    slot_ids = flat_ids * capacity + position
    slot_range = jnp.arange(experts * capacity, dtype=jnp.int32)
    selected = slot_range[:, None] == slot_ids[None, :]
    placement = jnp.any(
        selected.reshape(experts * capacity, quarter_rows, top_count), axis=2
    ).astype(jnp.bfloat16)
    send_rows = jnp.dot(placement, normed, preferred_element_type=jnp.float32).astype(jnp.bfloat16)
    send_rows = send_rows.reshape(ep_size, exp_local * capacity, model_width)
    received = lax.all_to_all(send_rows, "ep", split_axis=0, concat_axis=0, tiled=True)
    received = received.reshape(ep_size, exp_local, capacity, model_width)
    slots = ep_size * exp_local * capacity
    rows = received.reshape(slots, model_width)
    down_full = jnp.concatenate([piece.reshape(-1, model_width) for _, piece in pieces], axis=0)
    activated = []
    for gate_up_piece, _ in pieces:
        both = jnp.dot(
            rows, gate_up_piece.reshape(-1, model_width).T, preferred_element_type=jnp.float32
        ).reshape(slots, 2, -1)
        activated.append((jax.nn.silu(both[:, 0]) * both[:, 1]).astype(jnp.bfloat16))
    activated = jnp.concatenate(activated, axis=1)
    expert_out = jnp.dot(
        activated, down_full, preferred_element_type=jnp.float32
    ).astype(jnp.bfloat16)
    returned = lax.all_to_all(
        expert_out.reshape(ep_size, exp_local * capacity, model_width),
        "ep",
        split_axis=0,
        concat_axis=0,
        tiled=True,
    )
    returned = returned.reshape(experts * capacity, model_width)
    token_slots = slot_ids.reshape(quarter_rows, top_count)
    combine = jnp.zeros((quarter_rows, experts * capacity), jnp.float32)
    for choice_index in range(top_count):
        hit = slot_range[None, :] == token_slots[:, choice_index][:, None]
        combine = combine + jnp.where(hit, route_weights[:, choice_index : choice_index + 1], 0.0)
    combine_hi = combine.astype(jnp.bfloat16)
    combine_lo = (combine - combine_hi.astype(jnp.float32)).astype(jnp.bfloat16)
    picked = jnp.dot(
        jnp.concatenate([combine_hi, combine_lo], axis=0), returned, preferred_element_type=jnp.float32
    )
    mixture = picked[:quarter_rows] + picked[quarter_rows:]
    return (hidden + mixture).astype(jnp.bfloat16)


def solution(mesh):
    in_specs = (
        P("ep", "tp"),
        P("tp", None),
        P(("ep", "tp"), None),
        P(),
        P(("ep", "tp"), None),
        P(("ep", "tp"), None),
        P("ep", None, "tp", None),
        P("ep", "tp", None),
    )
    out_specs = P(("ep", "tp"), None)
    return jax.shard_map(layer, mesh=mesh, in_specs=in_specs, out_specs=out_specs, check_vma=False)
```

```python
import jax
import jax.numpy as jnp
from jax import lax
from jax.sharding import PartitionSpec as P


def gather_weights(w_gate_up, w_down):
    tp_size = lax.axis_size("tp")
    half = tp_size // 2
    far_pairs = [(j, j ^ half) for j in range(tp_size)]
    near_pairs = [(j, j ^ 1) for j in range(tp_size)]
    own = (w_gate_up, w_down)
    far_gu = lax.ppermute(w_gate_up, "tp", far_pairs)
    far_dn = lax.ppermute(w_down, "tp", far_pairs)
    far = (far_gu, far_dn)
    near_own = lax.ppermute(own, "tp", near_pairs)
    near_far = lax.ppermute(far, "tp", near_pairs)
    return [own, far, near_own, near_far]


def layer(context, wo_proj, residual, norm_gain, expert_ids, route_weights, w_gate_up, w_down):
    quarter_rows, model_width = residual.shape
    top_count = expert_ids.shape[1]
    exp_local = w_gate_up.shape[0]
    ep_size = lax.axis_size("ep")
    experts = exp_local * ep_size
    capacity = max(2, min(quarter_rows, 2 * quarter_rows * top_count // experts))
    pieces = gather_weights(w_gate_up, w_down)
    attn_part = jnp.dot(context, wo_proj, preferred_element_type=jnp.float32)
    tp_size = lax.axis_size("tp")
    shares = attn_part.astype(jnp.bfloat16).reshape(tp_size, quarter_rows, model_width)
    shares = lax.all_to_all(shares, "tp", split_axis=0, concat_axis=0, tiled=True)
    attn = jnp.sum(shares.astype(jnp.float32), axis=0)
    hidden = residual.astype(jnp.float32) + attn
    inverse_rms = lax.rsqrt(jnp.mean(hidden * hidden, axis=1, keepdims=True) + 1e-06)
    normed = (hidden * inverse_rms * norm_gain.astype(jnp.float32)).astype(jnp.bfloat16)
    flat_ids = expert_ids.reshape(-1)
    onehot = (flat_ids[:, None] == jnp.arange(experts, dtype=jnp.int32)[None, :]).astype(jnp.int32)
    before = jnp.cumsum(onehot, axis=0, dtype=jnp.int32) - onehot
    position = jnp.sum(before * onehot, axis=1, dtype=jnp.int32)
    slot_ids = flat_ids * capacity + position
    slot_range = jnp.arange(experts * capacity, dtype=jnp.int32)
    selected = slot_range[:, None] == slot_ids[None, :]
    placement = jnp.any(
        selected.reshape(experts * capacity, quarter_rows, top_count), axis=2
    ).astype(jnp.bfloat16)
    send_rows = jnp.dot(placement, normed, preferred_element_type=jnp.float32).astype(jnp.bfloat16)
    send_rows = send_rows.reshape(ep_size, exp_local * capacity, model_width)
    received = lax.all_to_all(send_rows, "ep", split_axis=0, concat_axis=0, tiled=True)
    received = received.reshape(ep_size, exp_local, capacity, model_width)
    slots = ep_size * exp_local * capacity
    rows = received.reshape(slots, model_width)
    down_full = jnp.concatenate([piece.reshape(-1, model_width) for _, piece in pieces], axis=0)
    activated = []
    for gate_up_piece, _ in pieces:
        both = jnp.dot(
            rows, gate_up_piece.reshape(-1, model_width).T, preferred_element_type=jnp.float32
        ).reshape(slots, 2, -1)
        activated.append((jax.nn.silu(both[:, 0]) * both[:, 1]).astype(jnp.bfloat16))
    activated = jnp.concatenate(activated, axis=1)
    expert_out = jnp.dot(
        activated, down_full, preferred_element_type=jnp.float32
    ).astype(jnp.bfloat16)
    returned = lax.all_to_all(
        expert_out.reshape(ep_size, exp_local * capacity, model_width),
        "ep",
        split_axis=0,
        concat_axis=0,
        tiled=True,
    )
    returned = returned.reshape(experts * capacity, model_width)
    token_slots = slot_ids.reshape(quarter_rows, top_count)
    combine = jnp.zeros((quarter_rows, experts * capacity), jnp.float32)
    for choice_index in range(top_count):
        hit = slot_range[None, :] == token_slots[:, choice_index][:, None]
        combine = combine + jnp.where(hit, route_weights[:, choice_index : choice_index + 1], 0.0)
    combine_hi = combine.astype(jnp.bfloat16)
    combine_lo = (combine - combine_hi.astype(jnp.float32)).astype(jnp.bfloat16)
    picked = jnp.dot(
        jnp.concatenate([combine_hi, combine_lo], axis=0), returned, preferred_element_type=jnp.float32
    )
    mixture = picked[:quarter_rows] + picked[quarter_rows:]
    return (hidden + mixture).astype(jnp.bfloat16)


def solution(mesh):
    in_specs = (
        P("ep", "tp"),
        P("tp", None),
        P(("ep", "tp"), None),
        P(),
        P(("ep", "tp"), None),
        P(("ep", "tp"), None),
        P("ep", None, "tp", None),
        P("ep", "tp", None),
    )
    out_specs = P(("ep", "tp"), None)
    return jax.shard_map(layer, mesh=mesh, in_specs=in_specs, out_specs=out_specs, check_vma=False)
```

```python
import jax
import jax.numpy as jnp
from jax import lax
from jax.sharding import PartitionSpec as P


def gather_weights(w_gate_up, w_down):
    tp_size = lax.axis_size("tp")
    half = tp_size // 2
    far_pairs = [(j, j ^ half) for j in range(tp_size)]
    near_pairs = [(j, j ^ 1) for j in range(tp_size)]
    own = (w_gate_up, w_down)
    far_gu = lax.ppermute(w_gate_up, "tp", far_pairs)
    far_dn = lax.ppermute(w_down, "tp", far_pairs)
    far = (far_gu, far_dn)
    near_own = lax.ppermute(own, "tp", near_pairs)
    near_far = lax.ppermute(far, "tp", near_pairs)
    return [own, far, near_own, near_far]


def layer(context, wo_proj, residual, norm_gain, expert_ids, route_weights, w_gate_up, w_down):
    quarter_rows, model_width = residual.shape
    top_count = expert_ids.shape[1]
    exp_local = w_gate_up.shape[0]
    ep_size = lax.axis_size("ep")
    experts = exp_local * ep_size
    capacity = max(2, min(quarter_rows, 2 * quarter_rows * top_count // experts))
    pieces = gather_weights(w_gate_up, w_down)
    attn_part = jnp.dot(context, wo_proj, preferred_element_type=jnp.float32)
    tp_size = lax.axis_size("tp")
    shares = attn_part.astype(jnp.bfloat16).reshape(tp_size, quarter_rows, model_width)
    shares = lax.all_to_all(shares, "tp", split_axis=0, concat_axis=0, tiled=True)
    attn = jnp.sum(shares.astype(jnp.float32), axis=0)
    hidden = residual.astype(jnp.float32) + attn
    inverse_rms = lax.rsqrt(jnp.mean(hidden * hidden, axis=1, keepdims=True) + 1e-06)
    normed = (hidden * inverse_rms * norm_gain.astype(jnp.float32)).astype(jnp.bfloat16)
    flat_ids = expert_ids.reshape(-1)
    onehot = (flat_ids[:, None] == jnp.arange(experts, dtype=jnp.int32)[None, :]).astype(jnp.int32)
    before = jnp.cumsum(onehot, axis=0, dtype=jnp.int32) - onehot
    position = jnp.sum(before * onehot, axis=1, dtype=jnp.int32)
    slot_ids = flat_ids * capacity + position
    slot_range = jnp.arange(experts * capacity, dtype=jnp.int32)
    selected = slot_range[:, None] == slot_ids[None, :]
    placement = jnp.any(
        selected.reshape(experts * capacity, quarter_rows, top_count), axis=2
    ).astype(jnp.bfloat16)
    send_rows = jnp.dot(placement, normed, preferred_element_type=jnp.float32).astype(jnp.bfloat16)
    send_rows = send_rows.reshape(ep_size, exp_local * capacity, model_width)
    received = lax.all_to_all(send_rows, "ep", split_axis=0, concat_axis=0, tiled=True)
    received = received.reshape(ep_size, exp_local, capacity, model_width)
    slots = ep_size * exp_local * capacity
    rows = received.reshape(slots, model_width)
    activated = []
    for gate_up_piece, _ in pieces:
        both = jnp.dot(
            rows, gate_up_piece.reshape(-1, model_width).T, preferred_element_type=jnp.float32
        ).reshape(slots, 2, -1)
        activated.append((jax.nn.silu(both[:, 0]) * both[:, 1]).astype(jnp.bfloat16))
    downs = [piece.reshape(-1, model_width) for _, piece in pieces]
    early_out = jnp.dot(
        jnp.concatenate([activated[0], activated[2]], axis=1),
        jnp.concatenate([downs[0], downs[2]], axis=0),
        preferred_element_type=jnp.float32,
    )
    late_out = jnp.dot(
        jnp.concatenate([activated[1], activated[3]], axis=1),
        jnp.concatenate([downs[1], downs[3]], axis=0),
        preferred_element_type=jnp.float32,
    )
    expert_out = (early_out + late_out).astype(jnp.bfloat16)
    returned = lax.all_to_all(
        expert_out.reshape(ep_size, exp_local * capacity, model_width),
        "ep",
        split_axis=0,
        concat_axis=0,
        tiled=True,
    )
    returned = returned.reshape(experts * capacity, model_width)
    token_slots = slot_ids.reshape(quarter_rows, top_count)
    combine = jnp.zeros((quarter_rows, experts * capacity), jnp.float32)
    for choice_index in range(top_count):
        hit = slot_range[None, :] == token_slots[:, choice_index][:, None]
        combine = combine + jnp.where(hit, route_weights[:, choice_index : choice_index + 1], 0.0)
    combine_hi = combine.astype(jnp.bfloat16)
    combine_lo = (combine - combine_hi.astype(jnp.float32)).astype(jnp.bfloat16)
    picked = jnp.dot(
        jnp.concatenate([combine_hi, combine_lo], axis=0), returned, preferred_element_type=jnp.float32
    )
    mixture = picked[:quarter_rows] + picked[quarter_rows:]
    return (hidden + mixture).astype(jnp.bfloat16)


def solution(mesh):
    in_specs = (
        P("ep", "tp"),
        P("tp", None),
        P(("ep", "tp"), None),
        P(),
        P(("ep", "tp"), None),
        P(("ep", "tp"), None),
        P("ep", None, "tp", None),
        P("ep", "tp", None),
    )
    out_specs = P(("ep", "tp"), None)
    return jax.shard_map(layer, mesh=mesh, in_specs=in_specs, out_specs=out_specs, check_vma=False)
```

```python
import jax
import jax.numpy as jnp
from jax import lax
from jax.sharding import PartitionSpec as P


def gather_weights(w_gate_up, w_down):
    tp_size = lax.axis_size("tp")
    half = tp_size // 2
    far_pairs = [(j, j ^ half) for j in range(tp_size)]
    near_pairs = [(j, j ^ 1) for j in range(tp_size)]
    own = (w_gate_up, w_down)
    far_gu = lax.ppermute(w_gate_up, "tp", far_pairs)
    far_dn = lax.ppermute(w_down, "tp", far_pairs)
    far = (far_gu, far_dn)
    near_own = lax.ppermute(own, "tp", near_pairs)
    near_far = lax.ppermute(far, "tp", near_pairs)
    return [own, far, near_own, near_far]


def layer(context, wo_proj, residual, norm_gain, expert_ids, route_weights, w_gate_up, w_down):
    quarter_rows, model_width = residual.shape
    top_count = expert_ids.shape[1]
    exp_local = w_gate_up.shape[0]
    ep_size = lax.axis_size("ep")
    experts = exp_local * ep_size
    capacity = max(2, min(quarter_rows, 2 * quarter_rows * top_count // experts))
    pieces = gather_weights(w_gate_up, w_down)
    attn_part = jnp.dot(context, wo_proj, preferred_element_type=jnp.float32)
    tp_size = lax.axis_size("tp")
    shares = attn_part.astype(jnp.bfloat16).reshape(tp_size, quarter_rows, model_width)
    shares = lax.all_to_all(shares, "tp", split_axis=0, concat_axis=0, tiled=True)
    attn = jnp.sum(shares.astype(jnp.float32), axis=0)
    hidden = residual.astype(jnp.float32) + attn
    inverse_rms = lax.rsqrt(jnp.mean(hidden * hidden, axis=1, keepdims=True) + 1e-06)
    normed = (hidden * inverse_rms * norm_gain.astype(jnp.float32)).astype(jnp.bfloat16)
    flat_ids = expert_ids.reshape(-1)
    onehot = (flat_ids[:, None] == jnp.arange(experts, dtype=jnp.int32)[None, :]).astype(jnp.int32)
    before = jnp.cumsum(onehot, axis=0, dtype=jnp.int32) - onehot
    position = jnp.sum(before * onehot, axis=1, dtype=jnp.int32)
    slot_ids = flat_ids * capacity + position
    slot_range = jnp.arange(experts * capacity, dtype=jnp.int32)
    selected = slot_range[:, None] == slot_ids[None, :]
    placement = jnp.any(
        selected.reshape(experts * capacity, quarter_rows, top_count), axis=2
    ).astype(jnp.bfloat16)
    send_rows = jnp.dot(placement, normed, preferred_element_type=jnp.float32).astype(jnp.bfloat16)
    send_rows = send_rows.reshape(ep_size, exp_local * capacity, model_width)
    received = lax.all_to_all(send_rows, "ep", split_axis=0, concat_axis=0, tiled=True)
    received = received.reshape(ep_size, exp_local, capacity, model_width)
    slots = ep_size * exp_local * capacity
    rows = received.reshape(slots, model_width)
    def gate_up_of(chosen):
        weight = jnp.concatenate([piece.reshape(-1, model_width) for piece in chosen], axis=0)
        both = jnp.dot(rows, weight.T, preferred_element_type=jnp.float32)
        both = both.reshape(slots, len(chosen), 2, -1)
        return (jax.nn.silu(both[:, :, 0]) * both[:, :, 1]).astype(jnp.bfloat16).reshape(slots, -1)

    early_act = gate_up_of([pieces[0][0], pieces[2][0]])
    late_act = gate_up_of([pieces[1][0], pieces[3][0]])
    downs = [piece.reshape(-1, model_width) for _, piece in pieces]
    early_out = jnp.dot(
        early_act,
        jnp.concatenate([downs[0], downs[2]], axis=0),
        preferred_element_type=jnp.float32,
    )
    late_out = jnp.dot(
        late_act,
        jnp.concatenate([downs[1], downs[3]], axis=0),
        preferred_element_type=jnp.float32,
    )
    expert_out = (early_out + late_out).astype(jnp.bfloat16)
    returned = lax.all_to_all(
        expert_out.reshape(ep_size, exp_local * capacity, model_width),
        "ep",
        split_axis=0,
        concat_axis=0,
        tiled=True,
    )
    returned = returned.reshape(experts * capacity, model_width)
    token_slots = slot_ids.reshape(quarter_rows, top_count)
    combine = jnp.zeros((quarter_rows, experts * capacity), jnp.float32)
    for choice_index in range(top_count):
        hit = slot_range[None, :] == token_slots[:, choice_index][:, None]
        combine = combine + jnp.where(hit, route_weights[:, choice_index : choice_index + 1], 0.0)
    combine_hi = combine.astype(jnp.bfloat16)
    combine_lo = (combine - combine_hi.astype(jnp.float32)).astype(jnp.bfloat16)
    picked = jnp.dot(
        jnp.concatenate([combine_hi, combine_lo], axis=0), returned, preferred_element_type=jnp.float32
    )
    mixture = picked[:quarter_rows] + picked[quarter_rows:]
    return (hidden + mixture).astype(jnp.bfloat16)


def solution(mesh):
    in_specs = (
        P("ep", "tp"),
        P("tp", None),
        P(("ep", "tp"), None),
        P(),
        P(("ep", "tp"), None),
        P(("ep", "tp"), None),
        P("ep", None, "tp", None),
        P("ep", "tp", None),
    )
    out_specs = P(("ep", "tp"), None)
    return jax.shard_map(layer, mesh=mesh, in_specs=in_specs, out_specs=out_specs, check_vma=False)
```
